768 devices in a mesh: freq: 96 (over z, x, y_hi), depth: 8 (over y_lo, core).
Axes of the slice: x: 4, y: 8 (y_hi: 2, y_lo: 4; y = y_hi * 4 + y_lo), z: 12, core: 2. Of those that a mesh axis runs over, the one named last changes fastest.
Arguments:
- slowness: float32 [8, 24576], P('depth', 'freq'), may hold values from 0.25 to 1
- freq_index: int32 [192], P('freq'), may hold values from 0 to 191, each once
- taps: float32 [192, 2, 11], replicated, may hold values from -1 to 1, as said below
- source_top: float32 [192, 8, 2, 24, 1024], P('freq', 'depth'), may hold values from -6 to 6
- adjoint_source: float32 [192, 8, 2, 24, 1024], P('freq', 'depth'), may hold values from -6 to 6
Outputs:
- gradient: float32 [8, 24576], P('depth', 'freq')
The draws below stay inside these ranges and needn't reach their ends.
Inputs may be any that keep to these rules, and one draw needn't show every extreme that they name: `freq_index`: each of 0 to 191 appears once. In each frequency the absolute values of the complex taps sum to at most 1.
All inputs are finite; a program needn't handle non-finite values.
Results may differ from the reference program's by a relative error of at most 0.0003.
Values sent between devices are 32-bit elements; how exact they have to be, the bound alone decides.
No kernel may reach another device: no remote copies, remote signals or barrier semaphores. Data moves between devices by JAX's collectives and lax.ppermute only.
A program may use at most 32 MiB of HBM per device.

```python
import math
import jax
import jax.numpy as jnp
from jax import lax

NX = 1024
YW = 24
TAPS = 11
FREQS = 192
NSEC = 8
NZ = 8


def draw_taps(key, part):
    keys = jax.random.split(key, 3)
    center = jax.random.uniform(keys[0], (FREQS, 1), jnp.float32, 0.7, 0.99)
    angle = jax.random.uniform(keys[1], (FREQS, TAPS), jnp.float32, -math.pi, math.pi)
    side = jax.random.uniform(keys[2], (FREQS, TAPS), jnp.float32, 0.5, 1.0) * (1.0 - center) / (TAPS - 1)
    middle = jnp.arange(TAPS) == TAPS // 2
    magnitude = jnp.where(middle[None, :], center, side)
    return jnp.stack([magnitude * jnp.cos(angle), magnitude * jnp.sin(angle)], axis=1).astype(jnp.float32)


def levels(stream_key, shape, cuts, smallest, largest):
    def one(dim, blocks):
        heights = jax.random.uniform(jax.random.fold_in(jax.random.fold_in(stream_key, 6), dim), (blocks,), jnp.float32, smallest / len(cuts), largest / len(cuts))
        return jnp.repeat(jnp.exp(heights), shape[dim] // blocks).reshape((-1,) + (1,) * (len(shape) - dim - 1))

    gain = one(*cuts[0])
    for cut in cuts[1:]:
        gain = gain * one(*cut)
    return gain


def gaussian(rng, dims, width, bound, pieces=(), kind=jnp.bfloat16):
    drawn = width * jax.random.normal(rng, dims, jnp.float32)
    if pieces:
        drawn = drawn * levels(rng, dims, pieces, -0.22, 0.18)
    return jnp.clip(drawn, -bound, bound).astype(kind)


def setup_inputs(seed: int = 0) -> dict:
    streams_of = jax.random.split(jax.random.key(seed), 6)
    slowness = jnp.clip(jnp.exp(math.log(1.0) - 1.3862944 * jax.random.uniform(streams_of[0], (NZ, YW * NX), jnp.float32) ** levels(streams_of[0], (NZ, YW * NX), ((0, 8), (1, 96)), -0.2, 0.2)), 0.25, 1.0)
    freq_index = jax.random.permutation(streams_of[1], FREQS).astype(jnp.int32)
    taps = draw_taps(jax.random.fold_in(streams_of[5], 71), 0)
    source_top = gaussian(streams_of[3], (FREQS, NSEC, 2, YW, NX), 1.0, 6.0, ((0, 96), (1, 8)), jnp.float32)
    adjoint_source = gaussian(streams_of[4], (FREQS, NZ, 2, YW, NX), 1.0, 6.0, ((0, 96), (1, 8)), jnp.float32)
    return dict(slowness=slowness, freq_index=freq_index, taps=taps, source_top=source_top, adjoint_source=adjoint_source)


def convolve(field_re, field_im, tap_re, tap_im, along, adjoint):
    along = field_re.ndim + along
    reach = tap_re.shape[-1] // 2
    extent = field_re.shape[along]
    widths = [(0, 0)] * field_re.ndim
    widths[along] = (reach, reach)
    padded_re = jnp.pad(field_re, widths)
    padded_im = jnp.pad(field_im, widths)
    out_re = jnp.zeros_like(field_re)
    out_im = jnp.zeros_like(field_im)
    for offset in range(2 * reach + 1):
        anchor = 2 * reach - offset if adjoint else offset
        shifted_re = lax.slice_in_dim(padded_re, anchor, anchor + extent, axis=along)
        shifted_im = lax.slice_in_dim(padded_im, anchor, anchor + extent, axis=along)
        coef_re = tap_re[..., offset][..., None, None]
        coef_im = tap_im[..., offset][..., None, None]
        if adjoint:
            out_re = out_re + coef_re * shifted_re + coef_im * shifted_im
            out_im = out_im + coef_re * shifted_im - coef_im * shifted_re
        else:
            out_re = out_re + coef_re * shifted_re - coef_im * shifted_im
            out_im = out_im + coef_re * shifted_im + coef_im * shifted_re
    return out_re, out_im


def forward_step(field_re, field_im, tap_re, tap_im, phase_cos, phase_sin):
    mid_re, mid_im = convolve(field_re, field_im, tap_re, tap_im, -1, False)
    mid_re, mid_im = convolve(mid_re, mid_im, tap_re, tap_im, -2, False)
    return phase_cos * mid_re - phase_sin * mid_im, phase_sin * mid_re + phase_cos * mid_im


def adjoint_step(field_re, field_im, tap_re, tap_im, phase_cos, phase_sin):
    mid_re = phase_cos * field_re + phase_sin * field_im
    mid_im = phase_cos * field_im - phase_sin * field_re
    mid_re, mid_im = convolve(mid_re, mid_im, tap_re, tap_im, -2, True)
    return convolve(mid_re, mid_im, tap_re, tap_im, -1, True)


def reference(slowness, freq_index, taps, source_top, adjoint_source):
    sections = source_top.shape[1]
    depth_total = slowness.shape[0]
    steps = depth_total // sections
    lines, cells = source_top.shape[3], source_top.shape[4]
    slow_grid = slowness.reshape(depth_total, lines, cells)
    count = taps.shape[0]

    def per_freq(total, inputs):
        index, source, adjoint = inputs
        angular = 8.0 * (index.astype(jnp.float32) + 1.0) / count
        tap_row = taps[index]
        tap_re, tap_im = tap_row[0], tap_row[1]
        phase = angular * slow_grid
        phase_cos = jnp.cos(phase)
        phase_sin = jnp.sin(phase)
        cos_sec = phase_cos.reshape(sections, steps, lines, cells)
        sin_sec = phase_sin.reshape(sections, steps, lines, cells)
        field_re, field_im = source[:, 0], source[:, 1]
        waves_re, waves_im = [], []
        for step in range(steps):
            field_re, field_im = forward_step(field_re, field_im, tap_re, tap_im, cos_sec[:, step], sin_sec[:, step])
            waves_re.append(field_re)
            waves_im.append(field_im)
        wave_re = jnp.stack(waves_re, axis=1).reshape(depth_total, lines, cells)
        wave_im = jnp.stack(waves_im, axis=1).reshape(depth_total, lines, cells)

        def backward(incoming, xs):
            q_re, q_im, w_re, w_im, c_part, s_part = xs
            mu_re = q_re + incoming[0]
            mu_im = q_im + incoming[1]
            term = angular * (mu_im * w_re - mu_re * w_im)
            return adjoint_step(mu_re, mu_im, tap_re, tap_im, c_part, s_part), term

        start = (jnp.zeros((lines, cells), jnp.float32), jnp.zeros((lines, cells), jnp.float32))
        _, terms = lax.scan(backward, start, (adjoint[:, 0], adjoint[:, 1], wave_re, wave_im, phase_cos, phase_sin), reverse=True)
        return total + terms, None

    total, _ = lax.scan(per_freq, jnp.zeros((depth_total, lines, cells), jnp.float32), (freq_index, source_top, adjoint_source))
    return (total / count).reshape(depth_total, lines * cells)
```

```python
import jax
import jax.numpy as jnp
from jax import lax
from jax.sharding import PartitionSpec as P


def from_behind(value, axis, steps):
    count = lax.axis_size(axis)
    leading, last = (max(0, -steps), min(count, count - steps))
    return lax.ppermute(value, axis, [(source, source + steps) for source in range(leading, last)])


def convolve(field_re, field_im, tap_re, tap_im, along, adjoint):
    along = field_re.ndim + along
    reach = tap_re.shape[-1] // 2
    extent = field_re.shape[along]
    widths = [(0, 0)] * field_re.ndim
    widths[along] = (reach, reach)
    padded_re = jnp.pad(field_re, widths)
    padded_im = jnp.pad(field_im, widths)
    out_re = jnp.zeros_like(field_re)
    out_im = jnp.zeros_like(field_im)
    for offset in range(2 * reach + 1):
        anchor = 2 * reach - offset if adjoint else offset
        shifted_re = lax.slice_in_dim(padded_re, anchor, anchor + extent, axis=along)
        shifted_im = lax.slice_in_dim(padded_im, anchor, anchor + extent, axis=along)
        coef_re = tap_re[..., offset][..., None, None]
        coef_im = tap_im[..., offset][..., None, None]
        if adjoint:
            out_re = out_re + coef_re * shifted_re + coef_im * shifted_im
            out_im = out_im + coef_re * shifted_im - coef_im * shifted_re
        else:
            out_re = out_re + coef_re * shifted_re - coef_im * shifted_im
            out_im = out_im + coef_re * shifted_im + coef_im * shifted_re
    return (out_re, out_im)


def forward_step(field_re, field_im, tap_re, tap_im, phase_cos, phase_sin):
    mid_re, mid_im = convolve(field_re, field_im, tap_re, tap_im, -1, False)
    mid_re, mid_im = convolve(mid_re, mid_im, tap_re, tap_im, -2, False)
    return (phase_cos * mid_re - phase_sin * mid_im, phase_sin * mid_re + phase_cos * mid_im)


def adjoint_step(field_re, field_im, tap_re, tap_im, phase_cos, phase_sin):
    mid_re = phase_cos * field_re + phase_sin * field_im
    mid_im = phase_cos * field_im - phase_sin * field_re
    mid_re, mid_im = convolve(mid_re, mid_im, tap_re, tap_im, -2, True)
    return convolve(mid_re, mid_im, tap_re, tap_im, -1, True)


def sweep(
    incoming, adj_re, adj_im, wave_re, wave_im, phase_cos, phase_sin, tap_re, tap_im, angular
):
    steps = adj_re.shape[1]
    carry = (incoming[:, 0], incoming[:, 1])
    terms = [None] * steps
    for step in reversed(range(steps)):
        mu_re = adj_re[:, step] + carry[0]
        mu_im = adj_im[:, step] + carry[1]
        terms[step] = jnp.sum(
            angular[:, None, None] * (mu_im * wave_re[:, step] - mu_re * wave_im[:, step]), axis=0
        )
        carry = adjoint_step(mu_re, mu_im, tap_re, tap_im, phase_cos[:, step], phase_sin[:, step])
    return (jnp.stack(carry, axis=1), jnp.stack(terms))


def on_device(slowness, freq_index, taps, source_top, adjoint_source):
    steps = slowness.shape[0]
    lines, cells = (source_top.shape[3], source_top.shape[4])
    groups = lax.axis_size("freq")
    block = slowness.shape[1]
    spread = jnp.broadcast_to(slowness.reshape(1, steps * block), (groups, steps * block))
    whole = lax.all_to_all(spread, "freq", 0, 0, tiled=True)
    whole = whole.reshape(groups, steps, block).swapaxes(0, 1).reshape(steps, lines, cells)
    count = taps.shape[0]
    lanes = freq_index.shape[0]
    onehot = (freq_index[:, None] == jnp.arange(count, dtype=jnp.int32)[None, :]).astype(
        jnp.float32
    )
    tap_table = jnp.dot(
        onehot,
        taps.reshape(count, -1),
        precision=lax.Precision.HIGHEST,
        preferred_element_type=jnp.float32,
    ).reshape(lanes, 2, -1)
    tap_re, tap_im = (tap_table[:, 0], tap_table[:, 1])
    angular = 8.0 * (freq_index.astype(jnp.float32) + 1.0) / count
    phase = angular[:, None, None, None] * whole[None]
    phase_cos = jnp.cos(phase)
    phase_sin = jnp.sin(phase)
    field_re, field_im = (source_top[:, 0, 0], source_top[:, 0, 1])
    waves_re, waves_im = ([], [])
    field_re, field_im = forward_step(
        field_re, field_im, tap_re, tap_im, phase_cos[:, 0], phase_sin[:, 0]
    )
    waves_re.append(field_re)
    waves_im.append(field_im)
    wave_re = jnp.stack(waves_re, axis=1)
    wave_im = jnp.stack(waves_im, axis=1)
    adj_re = adjoint_source[:, :, 0]
    adj_im = adjoint_source[:, :, 1]
    depth_count = lax.axis_size("depth")

    def segment(turn, received):
        top, _ = sweep(
            received,
            adj_re,
            adj_im,
            wave_re,
            wave_im,
            phase_cos,
            phase_sin,
            tap_re,
            tap_im,
            angular,
        )
        return from_behind(top, "depth", -1)

    received = lax.fori_loop(
        0, depth_count - 1, segment, jnp.zeros((lanes, 2, lines, cells), jnp.float32)
    )
    _, image = sweep(
        received, adj_re, adj_im, wave_re, wave_im, phase_cos, phase_sin, tap_re, tap_im, angular
    )
    parts = image.reshape(steps, groups, block).swapaxes(0, 1).reshape(groups, steps * block)
    parts = lax.all_to_all(parts, "freq", 0, 0, tiled=True)
    return jnp.sum(parts, axis=0).reshape(steps, block) / count


def solution(mesh):
    in_specs = (
        P("depth", "freq"),
        P("freq"),
        P(),
        P("freq", "depth", None, None, None),
        P("freq", "depth", None, None, None),
    )
    out_specs = P("depth", "freq")
    return jax.shard_map(
        on_device, mesh=mesh, in_specs=in_specs, out_specs=out_specs, check_vma=False
    )
```

```python
import functools
import jax
import jax.numpy as jnp
from jax import lax
from jax.experimental import pallas as pl
from jax.experimental.pallas import tpu as pltpu
from jax.sharding import PartitionSpec as P

CORES = 2
MARGIN = 64
VMEM = pl.BlockSpec(memory_space=pltpu.VMEM)
SMEM = pl.BlockSpec(memory_space=pltpu.SMEM)


def call(kernel, outs, in_specs, scratch=(), flops=0, moved=0):
    shapes = [jax.ShapeDtypeStruct(s, jnp.float32) for s in outs]
    return pl.pallas_call(
        kernel,
        out_shape=shapes if len(shapes) > 1 else shapes[0],
        in_specs=in_specs,
        out_specs=[VMEM] * len(shapes) if len(shapes) > 1 else VMEM,
        scratch_shapes=list(scratch),
        compiler_params=pltpu.CompilerParams(vmem_limit_bytes=40 << 20),
        cost_estimate=pl.CostEstimate(flops=flops, bytes_accessed=moved, transcendentals=0),
    )


def sincos(x):
    k = jnp.floor(x * 0.6366197723675814 + 0.5)
    r = x - k * 1.5703125
    r = r - k * 4.837512969970703e-4
    r = r - k * 7.549789948768648e-8
    r2 = r * r
    s = r + r * r2 * (-1.6666654611e-1 + r2 * (8.3321608736e-3 + r2 * -1.9515295891e-4))
    c = 1.0 - 0.5 * r2 + r2 * r2 * (
        4.166664568298827e-2 + r2 * (-1.388731625493765e-3 + r2 * 2.443315711809948e-5)
    )
    q = k.astype(jnp.int32)
    odd = (q & 1) == 1
    sin = jnp.where(odd, c, s)
    cos = jnp.where(odd, s, c)
    sin = jnp.where((q & 2) == 2, -sin, sin)
    cos = jnp.where(((q + 1) & 2) == 2, -cos, cos)
    return sin, cos


def along_x(re, im, taps, adjoint):
    width = re.shape[-1]
    count = len(taps)
    reach = count // 2
    out_re = out_im = None
    for k, (a, b) in enumerate(taps):
        shift = (reach - k) if not adjoint else (k - reach)
        s_re = pltpu.roll(re, shift % width, 1) if shift else re
        s_im = pltpu.roll(im, shift % width, 1) if shift else im
        if adjoint:
            t_re, t_im = a * s_re + b * s_im, a * s_im - b * s_re
        else:
            t_re, t_im = a * s_re - b * s_im, a * s_im + b * s_re
        out_re = t_re if out_re is None else out_re + t_re
        out_im = t_im if out_im is None else out_im + t_im
    return out_re, out_im


def along_y(ref, lines, tile, taps, adjoint):
    count = len(taps)
    reach = count // 2
    lanes = pl.ds(tile * 128, 128)
    out_re = out_im = None
    for k, (a, b) in enumerate(taps):
        first = 8 + ((k - reach) if not adjoint else (reach - k))
        s_re = ref[0, pl.ds(first, lines), lanes]
        s_im = ref[1, pl.ds(first, lines), lanes]
        if adjoint:
            t_re, t_im = a * s_re + b * s_im, a * s_im - b * s_re
        else:
            t_re, t_im = a * s_re - b * s_im, a * s_im + b * s_re
        out_re = t_re if out_re is None else out_re + t_re
        out_im = t_im if out_im is None else out_im + t_im
    return out_re, out_im


def read_taps(tap_ref, count):
    return [(tap_ref[k], tap_ref[count + k]) for k in range(count)]


def pack_kernel(quarters, where_ref, adj_ref, src_ref, got_ref, *refs):
    outs, pad_ref = refs[:-1], refs[-1]
    core, quarter = where_ref[0], where_ref[1]
    cells = adj_ref.shape[-1]
    lines = adj_ref.shape[-2]
    width = cells // quarters
    for zz in range(2):
        for n in range(4):
            pad_ref[zz, n, :, :128] = jnp.zeros((lines, 128), jnp.float32)
            pad_ref[zz, n, :, 128 + cells :] = jnp.zeros((lines, 128), jnp.float32)
    for part in range(2):
        pad_ref[core, part, :, 128 : 128 + cells] = adj_ref[core, part]
        pad_ref[core, 2 + part, :, 128 : 128 + cells] = src_ref[core, part]
        pad_ref[1 - core, part, :, 128 : 128 + cells] = got_ref[0, part]
        pad_ref[1 - core, 2 + part, :, 128 : 128 + cells] = got_ref[1, part]
    for k, out_ref in enumerate(outs):
        aim = lax.rem(quarter + k, quarters)
        lanes = pl.ds(pl.multiple_of(aim * width, 128), width + 256)
        for zz in range(2):
            for n in range(4):
                wide = pad_ref[zz, n, :, lanes]
                wide = pltpu.roll(wide, width + 256 - (128 - MARGIN), 1)
                out_ref[zz, n] = wide[:, : width + 2 * MARGIN]


def forward_kernel(quarters, count, where_ref, tap_ref, *refs):
    ins, (adj_ref, mid_ref), pad_ref = refs[:quarters], refs[quarters : quarters + 2], refs[-1]
    quarter = where_ref[1]
    taps = read_taps(tap_ref, count)
    lines, span = ins[0].shape[-2], ins[0].shape[-1]
    for part in range(2):
        pad_ref[part, :8] = jnp.zeros((8, span), jnp.float32)
        pad_ref[part, 8 + lines :] = jnp.zeros((8, span), jnp.float32)
    for k, in_ref in enumerate(ins):
        chip = lax.rem(quarter + quarters - k, quarters)
        for zz in range(2):
            z = chip * 2 + zz
            for part in range(2):
                adj_ref[z, part] = in_ref[zz, part]
            for row in range(0, lines, 8):
                rows = pl.ds(row, min(8, lines - row))
                re, im = along_x(in_ref[zz, 2, rows], in_ref[zz, 3, rows], taps, False)
                pad_ref[0, pl.ds(8 + row, re.shape[0])] = re
                pad_ref[1, pl.ds(8 + row, re.shape[0])] = im
            for tile in range(span // 128):
                re, im = along_y(pad_ref, lines, tile, taps, False)
                mid_ref[z, 0, :, tile * 128 : tile * 128 + 128] = re
                mid_ref[z, 1, :, tile * 128 : tile * 128 + 128] = im


def slow_kernel(quarters, in_ref, out_ref, pad_ref, *half_refs):
    width = in_ref.shape[-1]
    lines = in_ref.shape[0] // quarters
    cells = width * quarters
    pad_ref[:, :128] = jnp.zeros((lines, 128), jnp.float32)
    pad_ref[:, 128 + cells :] = jnp.zeros((lines, 128), jnp.float32)
    for n in range(width // 128):
        half_refs[n][...] = in_ref[:, n * 128 : n * 128 + 128]
    for c in range(quarters):
        for n in range(width // 128):
            first = 128 + c * width + n * 128
            pad_ref[:, first : first + 128] = half_refs[n][pl.ds(c, lines, stride=quarters), :]
    for c in range(quarters):
        wide = pad_ref[:, c * width : c * width + width + 256]
        wide = pltpu.roll(wide, width + 256 - (128 - MARGIN), 1)[:, : width + 2 * MARGIN]
        for core in range(CORES):
            out_ref[c * CORES + core] = wide


def chain_kernel(
    quarters, cells, count, where_ref, omega_ref, tap_ref, slow_ref, adj_ref, mid_ref, out_ref, mu_ref, pad_ref
):
    quarter = where_ref[1]
    omega = omega_ref[0]
    taps = read_taps(tap_ref, count)
    steps, lines, span = slow_ref.shape
    width = cells // quarters
    for part in range(2):
        pad_ref[part, :8] = jnp.zeros((8, span), jnp.float32)
        pad_ref[part, 8 + lines :] = jnp.zeros((8, span), jnp.float32)
        mu_ref[part] = jnp.zeros((lines, span), jnp.float32)
    for z in reversed(range(steps)):
        for row in range(0, lines, 8):
            many = min(8, lines - row)
            rows = pl.ds(row, many)
            mu_re = adj_ref[z, 0, rows] + mu_ref[0, rows]
            mu_im = adj_ref[z, 1, rows] + mu_ref[1, rows]
            sin, cos = sincos(omega * slow_ref[z, rows])
            mid_re, mid_im = mid_ref[z, 0, rows], mid_ref[z, 1, rows]
            wave_re = cos * mid_re - sin * mid_im
            wave_im = sin * mid_re + cos * mid_im
            term = omega * (mu_im * wave_re - mu_re * wave_im)
            out_ref[z, rows] = pltpu.roll(term, span - MARGIN, 1)[:, :width]
            if z:
                pad_ref[0, pl.ds(8 + row, many)] = cos * mu_re + sin * mu_im
                pad_ref[1, pl.ds(8 + row, many)] = cos * mu_im - sin * mu_re
        if z:
            for tile in range(span // 128):
                re, im = along_y(pad_ref, lines, tile, taps, True)
                mu_ref[0, :, tile * 128 : tile * 128 + 128] = re
                mu_ref[1, :, tile * 128 : tile * 128 + 128] = im
            for row in range(0, lines, 8):
                many = min(8, lines - row)
                rows = pl.ds(row, many)
                column = lax.broadcasted_iota(jnp.int32, (many, span), 1) + (quarter * width - MARGIN)
                inside = (column >= 0) & (column < cells)
                re, im = along_x(mu_ref[0, rows], mu_ref[1, rows], taps, True)
                mu_ref[0, rows] = jnp.where(inside, re, 0.0)
                mu_ref[1, rows] = jnp.where(inside, im, 0.0)


def regroup_kernel(quarters, in_ref, out_ref, *half_refs):
    lines, width = in_ref.shape[1], in_ref.shape[2]
    for c in range(quarters):
        both = in_ref[CORES * c] + in_ref[CORES * c + 1]
        for n in range(width // 128):
            half_refs[n][pl.ds(c, lines, stride=quarters), :] = both[:, n * 128 : n * 128 + 128]
    for n in range(width // 128):
        out_ref[:, n * 128 : n * 128 + 128] = half_refs[n][...]


def on_device(slowness, freq_index, taps, source_top, adjoint_source):
    lines, cells = source_top.shape[3], source_top.shape[4]
    groups, sections = lax.axis_size("freq"), lax.axis_size("depth")
    block = slowness.shape[1]
    quarters = sections // CORES
    width = cells // quarters
    span = width + 2 * MARGIN
    count, points = taps.shape[0], taps.shape[2]

    depth = lax.axis_index("depth")
    core, quarter = depth % CORES, depth // CORES
    where = jnp.stack([core, quarter]).astype(jnp.int32)
    chosen = lax.dynamic_index_in_dim(freq_index, core, 0, False)
    tap_row = lax.dynamic_index_in_dim(taps, chosen, 0, False).reshape(-1)
    omega = (8.0 * (chosen.astype(jnp.float32) + 1.0) / count).reshape(1)

    adj, src = adjoint_source[:, 0], source_top[:, 0]
    other = jnp.where(core == 0, jnp.stack([adj[1], src[1]]), jnp.stack([adj[0], src[0]]))
    got = lax.ppermute(other, "depth", [(d, d ^ 1) for d in range(sections)])

    spread = jnp.broadcast_to(slowness, (groups, block))
    plane = lax.all_to_all(spread, "freq", 0, 0, tiled=True)

    windows = call(
        functools.partial(pack_kernel, quarters),
        [(2, 4, lines, span)] * quarters,
        [SMEM, VMEM, VMEM, VMEM],
        [pltpu.VMEM((2, 4, lines, cells + 256), jnp.float32)],
        flops=1 << 20,
        moved=4 << 20,
    )(where, adj, src, got)
    arrived = [windows[0]]
    for k in range(1, quarters):
        hop = [(d, (d + CORES * k) % sections) for d in range(sections)]
        arrived.append(lax.ppermute(windows[k], "depth", hop))

    plane, *arrived = lax.optimization_barrier((plane, *arrived))
    slow = call(
        functools.partial(slow_kernel, quarters),
        [(sections, lines, span)],
        [VMEM],
        [
            pltpu.VMEM((lines, cells + 256), jnp.float32),
            *[pltpu.VMEM((groups, 128), jnp.float32)] * (block // 128),
        ],
        flops=1 << 18,
        moved=1 << 19,
    )(plane)
    slow = lax.all_to_all(slow, "depth", 0, 0, tiled=True)

    adj_all, mid_all = call(
        functools.partial(forward_kernel, quarters, points),
        [(sections, 2, lines, span)] * 2,
        [SMEM, SMEM] + [VMEM] * quarters,
        [pltpu.VMEM((2, lines + 16, span), jnp.float32)],
        flops=1 << 24,
        moved=4 << 20,
    )(where, tap_row, *arrived)

    image = call(
        functools.partial(chain_kernel, quarters, cells, points),
        [(sections, lines, width)],
        [SMEM, SMEM, SMEM, VMEM, VMEM, VMEM],
        [
            pltpu.VMEM((2, lines, span), jnp.float32),
            pltpu.VMEM((2, lines + 16, span), jnp.float32),
        ],
        flops=1 << 25,
        moved=4 << 20,
    )(where, omega, tap_row, slow, adj_all, mid_all)

    image = lax.all_to_all(image, "depth", 0, 0, tiled=True)
    rows = call(
        functools.partial(regroup_kernel, quarters),
        [(groups, block)],
        [VMEM],
        [pltpu.VMEM((groups, 128), jnp.float32)] * (block // 128),
        flops=1 << 17,
        moved=1 << 19,
    )(image)
    rows = lax.all_to_all(rows, "freq", 0, 0, tiled=True)
    return jnp.sum(rows, axis=0, keepdims=True) / count


def solution(mesh):
    in_specs = (
        P("depth", "freq"),
        P("freq"),
        P(),
        P("freq", "depth", None, None, None),
        P("freq", "depth", None, None, None),
    )
    out_specs = P("depth", "freq")
    return jax.shard_map(
        on_device, mesh=mesh, in_specs=in_specs, out_specs=out_specs, check_vma=False
    )
```

```python
import functools
import jax
import jax.numpy as jnp
from jax import lax
from jax.experimental import pallas as pl
from jax.experimental.pallas import tpu as pltpu
from jax.sharding import PartitionSpec as P

CORES = 2
MARGIN = 64
VMEM = pl.BlockSpec(memory_space=pltpu.VMEM)
SMEM = pl.BlockSpec(memory_space=pltpu.SMEM)
ANY = pl.BlockSpec(memory_space=pl.ANY)


def call(kernel, outs, in_specs, scratch=(), flops=0, moved=0):
    shapes = [jax.ShapeDtypeStruct(s, jnp.float32) for s in outs]
    return pl.pallas_call(
        kernel,
        out_shape=shapes if len(shapes) > 1 else shapes[0],
        in_specs=in_specs,
        out_specs=[VMEM] * len(shapes) if len(shapes) > 1 else VMEM,
        scratch_shapes=list(scratch),
        compiler_params=pltpu.CompilerParams(vmem_limit_bytes=40 << 20),
        cost_estimate=pl.CostEstimate(flops=flops, bytes_accessed=moved, transcendentals=0),
    )


def sincos(x):
    k = jnp.floor(x * 0.6366197723675814 + 0.5)
    r = x - k * 1.5703125
    r = r - k * 4.837512969970703e-4
    r = r - k * 7.549789948768648e-8
    r2 = r * r
    s = r + r * r2 * (-1.6666654611e-1 + r2 * (8.3321608736e-3 + r2 * -1.9515295891e-4))
    c = 1.0 - 0.5 * r2 + r2 * r2 * (
        4.166664568298827e-2 + r2 * (-1.388731625493765e-3 + r2 * 2.443315711809948e-5)
    )
    q = k.astype(jnp.int32)
    odd = (q & 1) == 1
    sin = jnp.where(odd, c, s)
    cos = jnp.where(odd, s, c)
    sin = jnp.where((q & 2) == 2, -sin, sin)
    cos = jnp.where(((q + 1) & 2) == 2, -cos, cos)
    return sin, cos


def along_x(re, im, taps, adjoint):
    width = re.shape[-1]
    count = len(taps)
    reach = count // 2
    out_re = out_im = None
    for k, (a, b) in enumerate(taps):
        shift = (reach - k) if not adjoint else (k - reach)
        s_re = pltpu.roll(re, shift % width, 1) if shift else re
        s_im = pltpu.roll(im, shift % width, 1) if shift else im
        if adjoint:
            t_re, t_im = a * s_re + b * s_im, a * s_im - b * s_re
        else:
            t_re, t_im = a * s_re - b * s_im, a * s_im + b * s_re
        out_re = t_re if out_re is None else out_re + t_re
        out_im = t_im if out_im is None else out_im + t_im
    return out_re, out_im


def along_y(ref, lines, tile, taps, adjoint):
    count = len(taps)
    reach = count // 2
    lanes = pl.ds(tile * 128, 128)
    out_re = out_im = None
    for k, (a, b) in enumerate(taps):
        first = 8 + ((k - reach) if not adjoint else (reach - k))
        s_re = ref[0, pl.ds(first, lines), lanes]
        s_im = ref[1, pl.ds(first, lines), lanes]
        if adjoint:
            t_re, t_im = a * s_re + b * s_im, a * s_im - b * s_re
        else:
            t_re, t_im = a * s_re - b * s_im, a * s_im + b * s_re
        out_re = t_re if out_re is None else out_re + t_re
        out_im = t_im if out_im is None else out_im + t_im
    return out_re, out_im


def read_taps(tap_ref, slot, count):
    first = slot * 2 * count
    return [(tap_ref[first + k], tap_ref[first + count + k]) for k in range(count)]


def pack_kernel(quarters, where_ref, adj_ref, src_ref, got_ref, _, *refs):
    outs, pad_ref = refs[:-1], refs[-1]
    core, quarter = where_ref[0], where_ref[1]
    cells = adj_ref.shape[-1]
    lines = adj_ref.shape[-2]
    width = cells // quarters
    for zz in range(2):
        for n in range(4):
            pad_ref[zz, n, :, :128] = jnp.zeros((lines, 128), jnp.float32)
            pad_ref[zz, n, :, 128 + cells :] = jnp.zeros((lines, 128), jnp.float32)
    for part in range(2):
        pad_ref[core, part, :, 128 : 128 + cells] = adj_ref[core, part]
        pad_ref[core, 2 + part, :, 128 : 128 + cells] = src_ref[core, part]
        pad_ref[1 - core, part, :, 128 : 128 + cells] = got_ref[0, part]
        pad_ref[1 - core, 2 + part, :, 128 : 128 + cells] = got_ref[1, part]
    for k, out_ref in enumerate(outs):
        aim = lax.rem(quarter + k, quarters)
        lanes = pl.ds(pl.multiple_of(aim * width, 128), width + 256)
        for zz in range(2):
            for n in range(4):
                wide = pad_ref[zz, n, :, lanes]
                wide = pltpu.roll(wide, width + 256 - (128 - MARGIN), 1)
                out_ref[zz, n] = wide[:, : width + 2 * MARGIN]


def forward_kernel(quarters, count, where_ref, tap_ref, *refs):
    ins, (adj_ref, mid_ref), pad_ref = refs[:quarters], refs[quarters : quarters + 2], refs[-1]
    quarter = where_ref[1]
    taps = read_taps(tap_ref, where_ref[0], count)
    lines, span = ins[0].shape[-2], ins[0].shape[-1]
    for part in range(2):
        pad_ref[part, :8] = jnp.zeros((8, span), jnp.float32)
        pad_ref[part, 8 + lines :] = jnp.zeros((8, span), jnp.float32)
    for k, in_ref in enumerate(ins):
        chip = lax.rem(quarter + quarters - k, quarters)
        for zz in range(2):
            z = chip * 2 + zz
            for part in range(2):
                adj_ref[z, part] = in_ref[zz, part]
            for row in range(0, lines, 8):
                rows = pl.ds(row, min(8, lines - row))
                re, im = along_x(in_ref[zz, 2, rows], in_ref[zz, 3, rows], taps, False)
                pad_ref[0, pl.ds(8 + row, re.shape[0])] = re
                pad_ref[1, pl.ds(8 + row, re.shape[0])] = im
            for tile in range(span // 128):
                re, im = along_y(pad_ref, lines, tile, taps, False)
                mid_ref[z, 0, :, tile * 128 : tile * 128 + 128] = re
                mid_ref[z, 1, :, tile * 128 : tile * 128 + 128] = im


def slow_kernel(quarters, in_ref, out_ref, pad_ref, *half_refs):
    width = in_ref.shape[-1]
    lines = in_ref.shape[0] // quarters
    cells = width * quarters
    pad_ref[:, :128] = jnp.zeros((lines, 128), jnp.float32)
    pad_ref[:, 128 + cells :] = jnp.zeros((lines, 128), jnp.float32)
    for n in range(width // 128):
        half_refs[n][...] = in_ref[:, n * 128 : n * 128 + 128]
    for c in range(quarters):
        for n in range(width // 128):
            first = 128 + c * width + n * 128
            pad_ref[:, first : first + 128] = half_refs[n][pl.ds(c, lines, stride=quarters), :]
    for c in range(quarters):
        wide = pad_ref[:, c * width : c * width + width + 256]
        wide = pltpu.roll(wide, width + 256 - (128 - MARGIN), 1)[:, : width + 2 * MARGIN]
        for core in range(CORES):
            out_ref[c * CORES + core] = wide


def chain_kernel(
    quarters, cells, freqs, count, where_ref, index_ref, tap_ref, slow_ref, adj_ref, mid_ref, out_ref, mu_ref, pad_ref
):
    quarter = where_ref[1]
    omega = 8.0 * (index_ref[where_ref[0]].astype(jnp.float32) + 1.0) / freqs
    taps = read_taps(tap_ref, where_ref[0], count)
    steps, lines, span = slow_ref.shape
    width = cells // quarters
    for part in range(2):
        pad_ref[part, :8] = jnp.zeros((8, span), jnp.float32)
        pad_ref[part, 8 + lines :] = jnp.zeros((8, span), jnp.float32)
        mu_ref[part] = jnp.zeros((lines, span), jnp.float32)
    for z in reversed(range(steps)):
        for row in range(0, lines, 8):
            many = min(8, lines - row)
            rows = pl.ds(row, many)
            mu_re = adj_ref[z, 0, rows] + mu_ref[0, rows]
            mu_im = adj_ref[z, 1, rows] + mu_ref[1, rows]
            sin, cos = sincos(omega * slow_ref[z, rows])
            mid_re, mid_im = mid_ref[z, 0, rows], mid_ref[z, 1, rows]
            wave_re = cos * mid_re - sin * mid_im
            wave_im = sin * mid_re + cos * mid_im
            term = omega * (mu_im * wave_re - mu_re * wave_im)
            out_ref[z, rows] = pltpu.roll(term, span - MARGIN, 1)[:, :width]
            if z:
                pad_ref[0, pl.ds(8 + row, many)] = cos * mu_re + sin * mu_im
                pad_ref[1, pl.ds(8 + row, many)] = cos * mu_im - sin * mu_re
        if z:
            for tile in range(span // 128):
                re, im = along_y(pad_ref, lines, tile, taps, True)
                mu_ref[0, :, tile * 128 : tile * 128 + 128] = re
                mu_ref[1, :, tile * 128 : tile * 128 + 128] = im
            for row in range(0, lines, 8):
                many = min(8, lines - row)
                rows = pl.ds(row, many)
                column = lax.broadcasted_iota(jnp.int32, (many, span), 1) + (quarter * width - MARGIN)
                inside = (column >= 0) & (column < cells)
                re, im = along_x(mu_ref[0, rows], mu_ref[1, rows], taps, True)
                mu_ref[0, rows] = jnp.where(inside, re, 0.0)
                mu_ref[1, rows] = jnp.where(inside, im, 0.0)


def regroup_kernel(quarters, in_ref, out_ref, *half_refs):
    lines, width = in_ref.shape[1], in_ref.shape[2]
    for c in range(quarters):
        both = in_ref[CORES * c] + in_ref[CORES * c + 1]
        for n in range(width // 128):
            half_refs[n][pl.ds(c, lines, stride=quarters), :] = both[:, n * 128 : n * 128 + 128]
    for n in range(width // 128):
        out_ref[:, n * 128 : n * 128 + 128] = half_refs[n][...]


def on_device(slowness, freq_index, taps, source_top, adjoint_source):
    lines, cells = source_top.shape[3], source_top.shape[4]
    groups, sections = lax.axis_size("freq"), lax.axis_size("depth")
    block = slowness.shape[1]
    quarters = sections // CORES
    width = cells // quarters
    span = width + 2 * MARGIN
    count, points = taps.shape[0], taps.shape[2]

    depth = lax.axis_index("depth")
    core, quarter = depth % CORES, depth // CORES
    where = jnp.stack([core, quarter]).astype(jnp.int32)
    onehot = freq_index[:, None] == jnp.arange(count, dtype=jnp.int32)[None, :]
    tap_rows = jnp.sum(jnp.where(onehot[:, :, None, None], taps[None], 0.0), axis=1).reshape(-1)

    adj, src = adjoint_source[:, 0], source_top[:, 0]
    other = jnp.stack([lax.dynamic_index_in_dim(a, 1 - core, 0, False) for a in (adj, src)])
    got = lax.ppermute(other, "depth", [(d, d ^ 1) for d in range(sections)])

    spread = jnp.broadcast_to(slowness[None], (groups, 1, block))
    plane = lax.all_to_all(spread, "freq", 0, 0, tiled=True).reshape(groups, block)

    windows = call(
        functools.partial(pack_kernel, quarters),
        [(2, 4, lines, span)] * quarters,
        [SMEM, VMEM, VMEM, VMEM, ANY],
        [pltpu.VMEM((2, 4, lines, cells + 256), jnp.float32)],
        flops=1 << 20,
        moved=4 << 20,
    )(where, adj, src, got, spread)
    arrived = [windows[0]]
    for k in range(1, quarters):
        hop = [(d, (d + CORES * k) % sections) for d in range(sections)]
        arrived.append(lax.ppermute(windows[k], "depth", hop))

    plane, *arrived = lax.optimization_barrier((plane, *arrived))
    slow = call(
        functools.partial(slow_kernel, quarters),
        [(sections, lines, span)],
        [VMEM],
        [
            pltpu.VMEM((lines, cells + 256), jnp.float32),
            *[pltpu.VMEM((groups, 128), jnp.float32)] * (block // 128),
        ],
        flops=1 << 18,
        moved=1 << 19,
    )(plane)
    slow = lax.all_to_all(slow, "depth", 0, 0, tiled=True)

    adj_all, mid_all = call(
        functools.partial(forward_kernel, quarters, points),
        [(sections, 2, lines, span)] * 2,
        [SMEM, SMEM] + [VMEM] * quarters,
        [pltpu.VMEM((2, lines + 16, span), jnp.float32)],
        flops=1 << 24,
        moved=4 << 20,
    )(where, tap_rows, *arrived)

    image = call(
        functools.partial(chain_kernel, quarters, cells, count, points),
        [(sections, lines, width)],
        [SMEM, SMEM, SMEM, VMEM, VMEM, VMEM],
        [
            pltpu.VMEM((2, lines, span), jnp.float32),
            pltpu.VMEM((2, lines + 16, span), jnp.float32),
        ],
        flops=1 << 25,
        moved=4 << 20,
    )(where, freq_index, tap_rows, slow, adj_all, mid_all)

    image = lax.all_to_all(image, "depth", 0, 0, tiled=True)
    rows = call(
        functools.partial(regroup_kernel, quarters),
        [(groups, block)],
        [VMEM],
        [pltpu.VMEM((groups, 128), jnp.float32)] * (block // 128),
        flops=1 << 17,
        moved=1 << 19,
    )(image)
    rows = lax.all_to_all(rows, "freq", 0, 0, tiled=True)
    return jnp.sum(rows, axis=0, keepdims=True) / count


def solution(mesh):
    in_specs = (
        P("depth", "freq"),
        P("freq"),
        P(),
        P("freq", "depth", None, None, None),
        P("freq", "depth", None, None, None),
    )
    out_specs = P("depth", "freq")
    return jax.shard_map(
        on_device, mesh=mesh, in_specs=in_specs, out_specs=out_specs, check_vma=False
    )
```

```python
import functools
import jax
import jax.numpy as jnp
from jax import lax
from jax.experimental import pallas as pl
from jax.experimental.pallas import tpu as pltpu
from jax.sharding import PartitionSpec as P

CORES = 2
MARGIN = 64
VMEM = pl.BlockSpec(memory_space=pltpu.VMEM)
SMEM = pl.BlockSpec(memory_space=pltpu.SMEM)
ANY = pl.BlockSpec(memory_space=pl.ANY)


def call(kernel, outs, in_specs, scratch=(), flops=0, moved=0):
    shapes = [jax.ShapeDtypeStruct(s, jnp.float32) for s in outs]
    return pl.pallas_call(
        kernel,
        out_shape=shapes if len(shapes) > 1 else shapes[0],
        in_specs=in_specs,
        out_specs=[VMEM] * len(shapes) if len(shapes) > 1 else VMEM,
        scratch_shapes=list(scratch),
        compiler_params=pltpu.CompilerParams(vmem_limit_bytes=40 << 20),
        cost_estimate=pl.CostEstimate(flops=flops, bytes_accessed=moved, transcendentals=0),
    )


def sincos(x):
    k = jnp.floor(x * 0.6366197723675814 + 0.5)
    r = x - k * 1.5703125
    r = r - k * 4.837512969970703e-4
    r = r - k * 7.549789948768648e-8
    r2 = r * r
    s = r + r * r2 * (-1.6666654611e-1 + r2 * (8.3321608736e-3 + r2 * -1.9515295891e-4))
    c = 1.0 - 0.5 * r2 + r2 * r2 * (
        4.166664568298827e-2 + r2 * (-1.388731625493765e-3 + r2 * 2.443315711809948e-5)
    )
    q = k.astype(jnp.int32)
    odd = (q & 1) == 1
    sin = jnp.where(odd, c, s)
    cos = jnp.where(odd, s, c)
    sin = jnp.where((q & 2) == 2, -sin, sin)
    cos = jnp.where(((q + 1) & 2) == 2, -cos, cos)
    return sin, cos


def along_x(re, im, taps, adjoint):
    width = re.shape[-1]
    count = len(taps)
    reach = count // 2
    out_re = out_im = None
    for k, (a, b) in enumerate(taps):
        shift = (reach - k) if not adjoint else (k - reach)
        s_re = pltpu.roll(re, shift % width, 1) if shift else re
        s_im = pltpu.roll(im, shift % width, 1) if shift else im
        if adjoint:
            t_re, t_im = a * s_re + b * s_im, a * s_im - b * s_re
        else:
            t_re, t_im = a * s_re - b * s_im, a * s_im + b * s_re
        out_re = t_re if out_re is None else out_re + t_re
        out_im = t_im if out_im is None else out_im + t_im
    return out_re, out_im


def along_y(ref, lines, tile, taps, adjoint):
    count = len(taps)
    reach = count // 2
    lanes = pl.ds(tile * 128, 128)
    out_re = out_im = None
    for k, (a, b) in enumerate(taps):
        first = 8 + ((k - reach) if not adjoint else (reach - k))
        s_re = ref[0, pl.ds(first, lines), lanes]
        s_im = ref[1, pl.ds(first, lines), lanes]
        if adjoint:
            t_re, t_im = a * s_re + b * s_im, a * s_im - b * s_re
        else:
            t_re, t_im = a * s_re - b * s_im, a * s_im + b * s_re
        out_re = t_re if out_re is None else out_re + t_re
        out_im = t_im if out_im is None else out_im + t_im
    return out_re, out_im


def read_taps(tap_ref, slot, count):
    first = slot * 2 * count
    return [(tap_ref[first + k], tap_ref[first + count + k]) for k in range(count)]


def pack_kernel(quarters, where_ref, adj_ref, src_ref, got_ref, _, *refs):
    outs, pad_ref = refs[:-1], refs[-1]
    core, quarter = where_ref[0], where_ref[1]
    cells = adj_ref.shape[-1]
    lines = adj_ref.shape[-2]
    width = cells // quarters
    for zz in range(2):
        for n in range(4):
            pad_ref[zz, n, :, :128] = jnp.zeros((lines, 128), jnp.float32)
            pad_ref[zz, n, :, 128 + cells :] = jnp.zeros((lines, 128), jnp.float32)
    for part in range(2):
        pad_ref[core, part, :, 128 : 128 + cells] = adj_ref[core, part]
        pad_ref[core, 2 + part, :, 128 : 128 + cells] = src_ref[core, part]
        pad_ref[1 - core, part, :, 128 : 128 + cells] = got_ref[0, part]
        pad_ref[1 - core, 2 + part, :, 128 : 128 + cells] = got_ref[1, part]
    for k, out_ref in enumerate(outs):
        aim = lax.rem(quarter + k, quarters)
        lanes = pl.ds(pl.multiple_of(aim * width, 128), width + 256)
        for zz in range(2):
            for n in range(4):
                wide = pad_ref[zz, n, :, lanes]
                wide = pltpu.roll(wide, width + 256 - (128 - MARGIN), 1)
                out_ref[zz, n] = wide[:, : width + 2 * MARGIN]


def forward_kernel(quarters, count, where_ref, tap_ref, *refs):
    ins, (adj_ref, mid_ref), pad_ref = refs[:quarters], refs[quarters : quarters + 2], refs[-1]
    quarter = where_ref[1]
    taps = read_taps(tap_ref, where_ref[0], count)
    lines, span = ins[0].shape[-2], ins[0].shape[-1]
    for part in range(2):
        pad_ref[part, :8] = jnp.zeros((8, span), jnp.float32)
        pad_ref[part, 8 + lines :] = jnp.zeros((8, span), jnp.float32)
    for k, in_ref in enumerate(ins):
        chip = lax.rem(quarter + quarters - k, quarters)
        for zz in range(2):
            z = chip * 2 + zz
            for part in range(2):
                adj_ref[z, part] = in_ref[zz, part]
            for row in range(0, lines, 8):
                rows = pl.ds(row, min(8, lines - row))
                re, im = along_x(in_ref[zz, 2, rows], in_ref[zz, 3, rows], taps, False)
                pad_ref[0, pl.ds(8 + row, re.shape[0])] = re
                pad_ref[1, pl.ds(8 + row, re.shape[0])] = im
            for tile in range(span // 128):
                re, im = along_y(pad_ref, lines, tile, taps, False)
                mid_ref[z, 0, :, tile * 128 : tile * 128 + 128] = re
                mid_ref[z, 1, :, tile * 128 : tile * 128 + 128] = im


def slow_kernel(quarters, in_ref, out_ref, pad_ref, *half_refs):
    width = in_ref.shape[-1]
    lines = in_ref.shape[0] // quarters
    cells = width * quarters
    pad_ref[:, :128] = jnp.zeros((lines, 128), jnp.float32)
    pad_ref[:, 128 + cells :] = jnp.zeros((lines, 128), jnp.float32)
    for n in range(width // 128):
        half_refs[n][...] = in_ref[:, n * 128 : n * 128 + 128]
    for c in range(quarters):
        for n in range(width // 128):
            first = 128 + c * width + n * 128
            pad_ref[:, first : first + 128] = half_refs[n][pl.ds(c, lines, stride=quarters), :]
    for c in range(quarters):
        wide = pad_ref[:, c * width : c * width + width + 256]
        wide = pltpu.roll(wide, width + 256 - (128 - MARGIN), 1)[:, : width + 2 * MARGIN]
        for core in range(CORES):
            out_ref[c * CORES + core] = wide


def chain_kernel(
    quarters, cells, freqs, count, where_ref, index_ref, tap_ref, slow_ref, adj_ref, mid_ref, out_ref, mu_ref, pad_ref
):
    quarter = where_ref[1]
    omega = 8.0 * (index_ref[where_ref[0]].astype(jnp.float32) + 1.0) / freqs
    taps = read_taps(tap_ref, where_ref[0], count)
    steps, lines, span = slow_ref.shape
    width = cells // quarters
    for part in range(2):
        pad_ref[part, :8] = jnp.zeros((8, span), jnp.float32)
        pad_ref[part, 8 + lines :] = jnp.zeros((8, span), jnp.float32)
        mu_ref[part] = jnp.zeros((lines, span), jnp.float32)
    for z in reversed(range(steps)):
        for row in range(0, lines, 8):
            many = min(8, lines - row)
            rows = pl.ds(row, many)
            mu_re = adj_ref[z, 0, rows] + mu_ref[0, rows]
            mu_im = adj_ref[z, 1, rows] + mu_ref[1, rows]
            sin, cos = sincos(omega * slow_ref[z, rows])
            mid_re, mid_im = mid_ref[z, 0, rows], mid_ref[z, 1, rows]
            wave_re = cos * mid_re - sin * mid_im
            wave_im = sin * mid_re + cos * mid_im
            term = omega * (mu_im * wave_re - mu_re * wave_im)
            out_ref[z, rows] = pltpu.roll(term, span - MARGIN, 1)[:, :width]
            if z:
                pad_ref[0, pl.ds(8 + row, many)] = cos * mu_re + sin * mu_im
                pad_ref[1, pl.ds(8 + row, many)] = cos * mu_im - sin * mu_re
        if z:
            for tile in range(span // 128):
                re, im = along_y(pad_ref, lines, tile, taps, True)
                mu_ref[0, :, tile * 128 : tile * 128 + 128] = re
                mu_ref[1, :, tile * 128 : tile * 128 + 128] = im
            for row in range(0, lines, 8):
                many = min(8, lines - row)
                rows = pl.ds(row, many)
                column = lax.broadcasted_iota(jnp.int32, (many, span), 1) + (quarter * width - MARGIN)
                inside = (column >= 0) & (column < cells)
                re, im = along_x(mu_ref[0, rows], mu_ref[1, rows], taps, True)
                mu_ref[0, rows] = jnp.where(inside, re, 0.0)
                mu_ref[1, rows] = jnp.where(inside, im, 0.0)


def regroup_kernel(quarters, in_ref, out_ref, *half_refs):
    lines, width = in_ref.shape[1], in_ref.shape[2]
    for c in range(quarters):
        both = in_ref[CORES * c] + in_ref[CORES * c + 1]
        for n in range(width // 128):
            half_refs[n][pl.ds(c, lines, stride=quarters), :] = both[:, n * 128 : n * 128 + 128]
    for n in range(width // 128):
        out_ref[:, n * 128 : n * 128 + 128] = half_refs[n][...]


def on_device(slowness, freq_index, taps, source_top, adjoint_source):
    lines, cells = source_top.shape[3], source_top.shape[4]
    groups, sections = lax.axis_size("freq"), lax.axis_size("depth")
    block = slowness.shape[1]
    quarters = sections // CORES
    width = cells // quarters
    span = width + 2 * MARGIN
    count, points = taps.shape[0], taps.shape[2]

    depth = lax.axis_index("depth")
    core, quarter = depth % CORES, depth // CORES
    where = jnp.stack([core, quarter]).astype(jnp.int32)
    onehot = freq_index[:, None] == jnp.arange(count, dtype=jnp.int32)[None, :]
    tap_rows = jnp.sum(jnp.where(onehot[:, :, None, None], taps[None], 0.0), axis=1).reshape(-1)

    adj, src = adjoint_source[:, 0], source_top[:, 0]
    other = jnp.stack([lax.dynamic_index_in_dim(a, 1 - core, 0, False) for a in (adj, src)])
    got = lax.ppermute(other, "depth", [(d, d ^ 1) for d in range(sections)])

    spread = jnp.broadcast_to(slowness[None], (groups, 1, block))
    plane = lax.all_to_all(spread, "freq", 0, 0, tiled=True).reshape(groups, block)

    windows = call(
        functools.partial(pack_kernel, quarters),
        [(2, 4, lines, span)] * quarters,
        [SMEM, VMEM, VMEM, VMEM, ANY],
        [pltpu.VMEM((2, 4, lines, cells + 256), jnp.float32)],
        flops=1 << 20,
        moved=4 << 20,
    )(where, adj, src, got, spread)
    arrived = [windows[0]] * quarters
    for k in sorted(range(1, quarters), key=lambda k: -min(k, quarters - k)):
        hop = [(d, (d + CORES * k) % sections) for d in range(sections)]
        arrived[k] = lax.ppermute(windows[k], "depth", hop)

    plane, *arrived = lax.optimization_barrier((plane, *arrived))
    slow = call(
        functools.partial(slow_kernel, quarters),
        [(sections, lines, span)],
        [VMEM],
        [
            pltpu.VMEM((lines, cells + 256), jnp.float32),
            *[pltpu.VMEM((groups, 128), jnp.float32)] * (block // 128),
        ],
        flops=1 << 18,
        moved=1 << 19,
    )(plane)
    slow = lax.all_to_all(slow, "depth", 0, 0, tiled=True)

    adj_all, mid_all = call(
        functools.partial(forward_kernel, quarters, points),
        [(sections, 2, lines, span)] * 2,
        [SMEM, SMEM] + [VMEM] * quarters,
        [pltpu.VMEM((2, lines + 16, span), jnp.float32)],
        flops=1 << 24,
        moved=4 << 20,
    )(where, tap_rows, *arrived)

    image = call(
        functools.partial(chain_kernel, quarters, cells, count, points),
        [(sections, lines, width)],
        [SMEM, SMEM, SMEM, VMEM, VMEM, VMEM],
        [
            pltpu.VMEM((2, lines, span), jnp.float32),
            pltpu.VMEM((2, lines + 16, span), jnp.float32),
        ],
        flops=1 << 25,
        moved=4 << 20,
    )(where, freq_index, tap_rows, slow, adj_all, mid_all)

    image = lax.all_to_all(image, "depth", 0, 0, tiled=True)
    rows = call(
        functools.partial(regroup_kernel, quarters),
        [(groups, block)],
        [VMEM],
        [pltpu.VMEM((groups, 128), jnp.float32)] * (block // 128),
        flops=1 << 17,
        moved=1 << 19,
    )(image)
    rows = lax.all_to_all(rows, "freq", 0, 0, tiled=True)
    return jnp.sum(rows, axis=0, keepdims=True) / count


def solution(mesh):
    in_specs = (
        P("depth", "freq"),
        P("freq"),
        P(),
        P("freq", "depth", None, None, None),
        P("freq", "depth", None, None, None),
    )
    out_specs = P("depth", "freq")
    return jax.shard_map(
        on_device, mesh=mesh, in_specs=in_specs, out_specs=out_specs, check_vma=False
    )
```
